768 devices in a mesh: gx: 8 (over x, core), gy: 96 (over y, z).
Axes of the slice: x: 4, y: 8, z: 12, core: 2. Of those that a mesh axis runs over, the one named last changes fastest.
Arguments:
- density: float32 [8, 1536, 1024], P(None, 'gy', 'gx'), may hold values from 0.5 to 2
- momentum: float32 [3, 8, 1536, 1024], P(None, None, 'gy', 'gx'), may hold values from -1.8 to 1.8
- energy: float32 [8, 1536, 1024], P(None, 'gy', 'gx'), may hold values from 2.5 to 4
- solid_flags: int32 [8, 1536, 1024], P(None, 'gy', 'gx'), may hold values from 0 to 1, as said below
Outputs:
- advanced_state: float32 [5, 8, 1536, 1024], P(None, None, 'gy', 'gx')
The draws below stay inside these ranges and needn't reach their ends.
Inputs may be any that keep to these rules, and one draw needn't show every extreme that they name: `solid_flags`: 1 marks a cell inside the vocal folds, 0 a fluid cell. In each plane of fixed z the folds occupy 1024 // 4 consecutive x positions, at the cells whose distance in y from a centre is at least an opening of 0 to 383 cells.
All inputs are finite; a program needn't handle non-finite values.
Results may differ from the reference program's by a relative error of at most 0.0003.
Values sent between devices are 32-bit elements; how exact they have to be, the bound alone decides.
No kernel may reach another device: no remote copies, remote signals or barrier semaphores. Data moves between devices by JAX's collectives and lax.ppermute only.
A program may use at most 32 MiB of HBM per device.

```python
import math
import jax
import jax.numpy as jnp
from jax import lax

NZ = 8
NX = 1024
NY = 1536


def draw_solid_flags(key, part):
    subkeys = jax.random.split(key, 3)
    opening = jax.random.randint(subkeys[0], (NZ, 1, 1), 0, NY // 4)
    center = jax.random.randint(subkeys[1], (NZ, 1, 1), NY // 2 - NY // 8, NY // 2 + NY // 8 + 1)
    inlet_start = jax.random.randint(subkeys[2], (NZ, 1, 1), 0, NX // 2)
    row_place = jnp.arange(NY).reshape(1, NY, 1)
    column_place = jnp.arange(NX).reshape(1, 1, NX)
    inside = (column_place >= inlet_start) & (column_place < inlet_start + NX // 4) & (jnp.abs(row_place - center) >= opening)
    return inside.astype(jnp.int32)


def level_of(own_key, dims, shards, least, high):
    gain, own = 1.0, jax.random.fold_in(own_key, 6)
    for dim, blocks in shards:
        heights = jnp.exp(jax.random.uniform(jax.random.fold_in(own, dim), (blocks,), jnp.float32, least / len(shards), high / len(shards)))
        gain = gain * jnp.repeat(heights, dims[dim] // blocks).reshape([-1 if axis == dim else 1 for axis in range(len(dims))])
    return gain


def noise(rng, dims, deviation, limit, cuts=(), dtype=jnp.bfloat16):
    array = deviation * jax.random.normal(rng, dims, jnp.float32)
    if cuts:
        array = array * level_of(rng, dims, cuts, -0.22, 0.18)
    return jnp.clip(array, -limit, limit).astype(dtype)


def setup_inputs(seed: int = 0) -> dict:
    streams_of = jax.random.split(jax.random.key(seed), 5)
    density = jnp.clip(jnp.exp(math.log(2.0) - 1.3862944 * jax.random.uniform(streams_of[0], (NZ, NY, NX), jnp.float32) ** level_of(streams_of[0], (NZ, NY, NX), ((1, 96), (2, 8)), -0.2, 0.2)), 0.5, 2.0)
    momentum = noise(streams_of[1], (3, NZ, NY, NX), 0.3, 1.8, ((2, 96), (3, 8)), jnp.float32)
    energy = jnp.clip(2.5 + 1.5 * jax.random.uniform(streams_of[2], (NZ, NY, NX), jnp.float32) ** level_of(streams_of[2], (NZ, NY, NX), ((1, 96), (2, 8)), -0.2, 0.2), 2.5, 4.0)
    solid_flags = draw_solid_flags(jax.random.fold_in(streams_of[4], 71), 0)
    return {"density": density, "momentum": momentum, "energy": energy, "solid_flags": solid_flags}


gas_gamma = 1.4
step_size = 0.1
filter_alpha = 0.4999

def fluxes(density, momentum, energy):
    velocity = momentum[0] / density
    kinetic = 0.5 * (momentum[0] * momentum[0] + momentum[1] * momentum[1] + momentum[2] * momentum[2]) / density
    pressure = (gas_gamma - 1.0) * (energy - kinetic)
    return jnp.stack([momentum[0], momentum[0] * velocity + pressure, momentum[1] * velocity, momentum[2] * velocity, (energy + pressure) * velocity])

def filter_weights():
    weight = filter_alpha
    return [(193.0 + 126.0 * weight) / 256.0, (105.0 + 302.0 * weight) / 256.0, 15.0 * (2.0 * weight - 1.0) / 64.0, 45.0 * (1.0 - 2.0 * weight) / 512.0, 5.0 * (2.0 * weight - 1.0) / 256.0, (1.0 - 2.0 * weight) / 512.0]

def derive_line(field_lines):
    length = field_lines.shape[-1]
    flattened = field_lines.reshape(-1, length)
    padded = jnp.pad(flattened, ((0, 0), (2, 2)))
    right_side = 7.0 / 9.0 * (padded[:, 3:length + 3] - padded[:, 1:length + 1]) + 1.0 / 36.0 * (padded[:, 4:length + 4] - padded[:, 0:length])
    position = jnp.arange(length)
    closure_start = 0.5 * (-5.0 * flattened[:, 0:1] + 4.0 * flattened[:, 1:2] + flattened[:, 2:3])
    closure_next = 0.75 * (flattened[:, 2:3] - flattened[:, 0:1])
    closure_penult = 0.75 * (flattened[:, length - 1:length] - flattened[:, length - 3:length - 2])
    closure_end = 0.5 * (5.0 * flattened[:, length - 1:length] - 4.0 * flattened[:, length - 2:length - 1] - flattened[:, length - 3:length - 2])
    right_side = jnp.where(position == 0, closure_start, right_side)
    right_side = jnp.where(position == 1, closure_next, right_side)
    right_side = jnp.where(position == length - 2, closure_penult, right_side)
    right_side = jnp.where(position == length - 1, closure_end, right_side)
    near_ends = (position == 1) | (position == length - 2)
    lower_band = jnp.where(position == length - 1, 2.0, jnp.where(near_ends, 0.25, 1.0 / 3.0))
    lower_band = jnp.where(position == 0, 0.0, lower_band).astype(jnp.float32)
    upper_band = jnp.where(position == 0, 2.0, jnp.where(near_ends, 0.25, 1.0 / 3.0))
    upper_band = jnp.where(position == length - 1, 0.0, upper_band).astype(jnp.float32)
    diagonal = jnp.ones((length,), jnp.float32)
    solved = lax.linalg.tridiagonal_solve(lower_band, diagonal, upper_band, right_side.T)
    return solved.T.reshape(field_lines.shape)

def filter_line(field_lines):
    length = field_lines.shape[1]
    columns = jnp.transpose(field_lines, (1, 0, 2)).reshape(length, -1)
    padded = jnp.pad(columns, ((5, 5), (0, 0)))
    weights = filter_weights()
    right_side = weights[0] * columns
    for distance in range(1, 6):
        right_side = right_side + 0.5 * weights[distance] * (padded[5 + distance:5 + distance + length] + padded[5 - distance:5 - distance + length])
    position = jnp.arange(length)
    interior = (position >= 5) & (position <= length - 6)
    right_side = jnp.where(interior[:, None], right_side, columns)
    coupling = jnp.where(interior, filter_alpha, 0.0).astype(jnp.float32)
    diagonal = jnp.ones((length,), jnp.float32)
    solved = lax.linalg.tridiagonal_solve(coupling, diagonal, coupling, right_side)
    return jnp.transpose(solved.reshape(length, field_lines.shape[0], field_lines.shape[2]), (1, 0, 2))

def reference(density, momentum, energy, solid_flags):
    fluid_cells = (1 - solid_flags).astype(jnp.float32)
    flux_fields = fluxes(density, momentum, energy)
    derivative = lax.map(derive_line, flux_fields)
    conserved = jnp.concatenate([density[None], momentum, energy[None]], axis=0)
    advanced = conserved - step_size * derivative
    advanced = jnp.concatenate([advanced[0:1], advanced[1:4] * fluid_cells, advanced[4:5]], axis=0)
    filtered = lax.map(filter_line, advanced)
    return jnp.concatenate([filtered[0:1], filtered[1:4] * fluid_cells, filtered[4:5]], axis=0)
```

```python
import functools
import math

import jax
import jax.numpy as jnp
import numpy as np
from jax import lax
from jax.experimental import pallas as pl
from jax.experimental.pallas import tpu as pltpu
from jax.sharding import PartitionSpec as P

gas_gamma = 1.4
step_size = 0.1
filter_alpha = 0.4999
reach = 5
inner = 12
exact = lax.Precision.HIGHEST


def derivative_matrix(length):
    left = np.eye(length)
    right = np.zeros((length, length))
    for i in range(2, length - 2):
        left[i, i - 1] = left[i, i + 1] = 1.0 / 3.0
        right[i, i + 1], right[i, i - 1] = 7.0 / 9.0, -7.0 / 9.0
        right[i, i + 2], right[i, i - 2] = 1.0 / 36.0, -1.0 / 36.0
    left[0, 1] = 2.0
    right[0, :3] = -2.5, 2.0, 0.5
    left[1, 0] = left[1, 2] = 0.25
    right[1, 0], right[1, 2] = -0.75, 0.75
    left[-2, -3] = left[-2, -1] = 0.25
    right[-2, -3], right[-2, -1] = -0.75, 0.75
    left[-1, -2] = 2.0
    right[-1, -3:] = -0.5, -2.0, 2.5
    return np.linalg.solve(left, right)


def streamwise_tables(parts, width):
    whole = derivative_matrix(parts * width)
    rows = [slice(p * width, (p + 1) * width) for p in range(parts)]
    own = np.stack([whole[rows[p], rows[p]].T for p in range(parts)])
    sends = np.zeros((parts, 8, width))
    applied = np.zeros((parts, 8, width))
    for p in range(parts):
        if p + 1 < parts:
            block = whole[rows[p + 1], rows[p]]
            sends[p, 0:2] = block[0:2]
            applied[p + 1, 0, 0] = 1.0
            applied[p + 1, 1, 1:] = block[1:, -1] / block[1, -1]
        if p > 0:
            block = whole[rows[p - 1], rows[p]]
            sends[p, 2], sends[p, 3] = block[-1], block[-2]
            applied[p - 1, 2, -1] = 1.0
            applied[p - 1, 3, :-1] = block[:-1, 0] / block[-2, 0]
    return (
        (-step_size * own).astype(np.float32),
        sends.astype(np.float32),
        (-step_size * applied).astype(np.float32),
    )


def correction_matrix(length):
    count = length - 2 * reach
    left = np.eye(count)
    index = np.arange(count - 1)
    left[index, index + 1] = left[index + 1, index] = filter_alpha
    right = np.zeros((count, length))
    scale = (1.0 - 2.0 * filter_alpha) / 1024.0
    for shift in range(-reach, reach + 1):
        right[np.arange(count), np.arange(count) + reach + shift] = (
            scale * (-1.0) ** shift * math.comb(10, reach + shift)
        )
    whole = np.zeros((length, length))
    whole[reach : length - reach] = np.linalg.solve(left, right)
    return whole


def transverse_tables(parts, width):
    length = parts * width
    whole = correction_matrix(length)
    eta = math.acosh(0.5 / filter_alpha)

    def falling(ahead, behind):
        last = length - reach
        sign = (-1.0) ** (ahead - behind)
        return sign * math.sinh((last - ahead) * eta) / math.sinh((last - behind) * eta)

    def rising(ahead, behind):
        sign = (-1.0) ** (ahead - behind)
        return sign * math.sinh((ahead - reach + 1) * eta) / math.sinh((behind - reach + 1) * eta)

    outer = parts // inner
    own = np.zeros((parts, width, width + 2 * reach))
    up = np.zeros((parts, width))
    down = np.zeros((parts, width))
    from_low = np.zeros((parts, width))
    from_high = np.zeros((parts, width))
    for p in range(parts):
        start, end = p * width, (p + 1) * width - 1
        cells = slice(start, end + 1)
        if p + 1 < parts:
            up[p] = whole[end + 1 + reach, cells] * falling(end + 1, end + 1 + reach)
        if p > 0:
            down[p] = whole[start - 1 - reach, cells] * rising(start - 1, start - 1 - reach)
        for row in range(start, end + 1):
            if reach <= row < length - reach:
                from_low[p, row - start] = falling(row, start)
                from_high[p, row - start] = rising(row, end)
    for p in range(parts):
        start, end = p * width, (p + 1) * width - 1
        cells = slice(start, end + 1)
        own[p, :, reach : reach + width] = whole[cells, cells]
        if p > 0:
            near = whole[cells, start - reach : start]
            own[p, :, :reach] = near - np.outer(from_low[p], up[p - 1, -reach:])
        if p + 1 < parts:
            near = whole[cells, end + 1 : end + 1 + reach]
            own[p, :, reach + width :] = near - np.outer(from_high[p], down[p + 1, :reach])
    within = np.zeros((parts, 4, inner))
    across = np.zeros((parts, 2, outer))
    for p in range(parts):
        group, place = divmod(p, inner)
        start, end = p * width, (p + 1) * width - 1
        low_edge, high_edge = group * inner * width - 1, (group + 1) * inner * width
        for k in range(inner):
            q = group * inner + k
            if k < place:
                within[p, 0, k] = falling(start, (q + 1) * width)
            if k > place:
                within[p, 1, k] = rising(end, q * width - 1)
            if group + 1 < outer:
                within[p, 2, k] = falling(high_edge, (q + 1) * width)
            if group > 0:
                within[p, 3, k] = rising(low_edge, q * width - 1)
        for other in range(outer):
            if other < group:
                across[p, 0, other] = falling(start, (other + 1) * inner * width)
            if other > group:
                across[p, 1, other] = rising(end, other * inner * width - 1)
    ends = np.stack([up, down], axis=1)
    last = np.concatenate(
        [
            own.reshape(parts, -1),
            from_low,
            from_high,
            across.reshape(parts, -1),
        ],
        axis=1,
    )
    return [packed(table) for table in (ends, within, last)]


def packed(table):
    parts = table.shape[0]
    flat = table.reshape(parts, -1)
    room = -(-flat.shape[1] // 128) * 128
    wide = np.zeros((parts, 1, room), np.float32)
    wide[:, 0, : flat.shape[1]] = flat
    return wide


def first_kernel(place, density, momentum, energy, flags, own, sends, partial, fluid, to_right, to_left, flux):
    planes, transverse = 8, 16
    cells = planes * transverse
    for j in range(transverse):
        picked = pl.ds(j, planes, stride=transverse)
        rho = density[picked, :]
        m0 = momentum[pl.ds(j, planes, stride=transverse), :]
        m1 = momentum[pl.ds(cells + j, planes, stride=transverse), :]
        m2 = momentum[pl.ds(2 * cells + j, planes, stride=transverse), :]
        total = energy[picked, :]
        row = pl.ds(j * planes, planes)
        fluid[row, :] = (1 - flags[picked, :]).astype(jnp.float32)
        inverse = 1.0 / rho
        velocity = m0 * inverse
        kinetic = 0.5 * (m0 * m0 + m1 * m1 + m2 * m2) * inverse
        pressure = (gas_gamma - 1.0) * (total - kinetic)
        fields = (
            m0,
            m0 * velocity + pressure,
            m1 * velocity,
            m2 * velocity,
            (total + pressure) * velocity,
        )
        for f, (held, moved) in enumerate(zip((rho, m0, m1, m2, total), fields)):
            at = pl.ds(f * cells + j * planes, planes)
            partial[at, :] = held
            flux[at, :] = moved
    lines = flux[...]
    sent = lax.dot_general(
        sends[0], lines, (((1,), (1,)), ((), ())), precision=exact, preferred_element_type=jnp.float32
    )
    to_right[...] = sent[0:2]
    to_left[...] = sent[2:4]
    partial[...] = partial[...] + jnp.dot(
        lines, own[0], precision=exact, preferred_element_type=jnp.float32
    )


def second_kernel(place, partial, fluid, before, after, applied, ends, advanced, summed, upper, lower):
    planes, transverse = 8, 16
    cells = planes * transverse
    count = partial.shape[0]
    received = jnp.concatenate(
        [before[...], after[...], jnp.zeros((4, count), jnp.float32)], axis=0
    )
    added = lax.dot_general(
        received, applied[0], (((0,), (0,)), ((), ())), precision=exact, preferred_element_type=jnp.float32
    )
    state = partial[...] + added
    mask = fluid[...]
    for f in range(5):
        part = state[f * cells : (f + 1) * cells]
        if 1 <= f <= 3:
            part = part * mask
        advanced[f * cells : (f + 1) * cells, :] = part
        low, high = None, None
        for j in range(transverse):
            row = part[j * planes : (j + 1) * planes]
            one, two = ends[0, 0, j] * row, ends[0, 0, transverse + j] * row
            low = one if low is None else low + one
            high = two if high is None else high + two
        summed[f * planes : (f + 1) * planes, :] = low
        summed[(5 + f) * planes : (6 + f) * planes, :] = high
        width = reach * planes
        upper[f * width : (f + 1) * width, :] = part[cells - width :]
        lower[f * width : (f + 1) * width, :] = part[:width]


def third_kernel(place, gathered, within, prefix, slab):
    lines = gathered.shape[1] // 2
    outer = slab.shape[0]
    group = place[1]
    sums = []
    for kind in range(4):
        side = kind % 2
        total = None
        for k in range(inner):
            term = within[0, 0, kind * inner + k] * gathered[k, side * lines : (side + 1) * lines, :]
            total = term if total is None else total + term
        sums.append(total)
    prefix[:lines, :] = sums[0]
    prefix[lines:, :] = sums[1]
    for other in range(outer):
        slab[other, :, :] = jnp.where(other > group, sums[2], sums[3])


def last_kernel(place, advanced, fluid, before, after, prefix, exchanged, table, result):
    planes, transverse = 8, 16
    cells = planes * transverse
    lines = 5 * planes
    outer = exchanged.shape[0]
    span = transverse + 2 * reach
    base = transverse * span
    low, high = prefix[:lines, :], prefix[lines:, :]
    for other in range(outer):
        low = low + table[0, 0, base + 2 * transverse + other] * exchanged[other]
        high = high + table[0, 0, base + 2 * transverse + outer + other] * exchanged[other]
    width = reach * planes

    def cell(f, k):
        if k < reach:
            return before[f * width + k * planes : f * width + (k + 1) * planes, :]
        k -= reach
        if k < transverse:
            return advanced[f * cells + k * planes : f * cells + (k + 1) * planes, :]
        k -= transverse
        return after[f * width + k * planes : f * width + (k + 1) * planes, :]

    for i in range(transverse):
        falls, rises = table[0, 0, base + i], table[0, 0, base + transverse + i]
        sums = [
            falls * low[f * planes : (f + 1) * planes] + rises * high[f * planes : (f + 1) * planes]
            for f in range(5)
        ]
        for k in range(span):
            if k < reach and i >= reach or k >= reach + transverse and i < transverse - reach:
                continue
            weight = table[0, 0, i * span + k]
            sums = [total + weight * cell(f, k) for f, total in enumerate(sums)]
        keep = fluid[i * planes : (i + 1) * planes, :]
        for f in range(5):
            value = cell(f, reach + i) - sums[f]
            if 1 <= f <= 3:
                value = value * keep
            result[pl.ds(f * cells + i, planes, stride=transverse), :] = value


def whole_block(shape):
    return pl.BlockSpec(shape, lambda i, place: (0,) * len(shape))


def picked_block(table, which, space=None):
    zeros = (0,) * (table.ndim - 1)
    shape = (1,) + table.shape[1:]
    if space is None:
        return pl.BlockSpec(shape, lambda i, place: (place[which],) + zeros)
    return pl.BlockSpec(shape, lambda i, place: (place[which],) + zeros, memory_space=space)


def call(kernel, name, place, arrays, tables, outs, scratch=()):
    in_specs = [whole_block(a.shape) for a in arrays]
    in_specs += [picked_block(table, which, space) for table, which, space in tables]
    shapes = [jax.ShapeDtypeStruct(shape, jnp.float32) for shape in outs]
    return pl.pallas_call(
        kernel,
        grid_spec=pltpu.PrefetchScalarGridSpec(
            num_scalar_prefetch=1,
            grid=(1,),
            in_specs=in_specs,
            out_specs=[whole_block(shape) for shape in outs],
            scratch_shapes=list(scratch),
        ),
        out_shape=shapes,
        name=name,
    )(place, *arrays, *[jnp.asarray(table) for table, _, _ in tables])


def body(tables, density, momentum, energy, solid_flags):
    own, sends, applied, ends, within, last = tables
    planes, transverse, width = density.shape
    cells = planes * transverse
    parts, columns = lax.axis_size("gy"), lax.axis_size("gx")
    outer = parts // inner
    gx, gy = lax.axis_index("gx"), lax.axis_index("gy")
    place = jnp.stack([gy, gy // inner, gx]).astype(jnp.int32)
    smem = pltpu.SMEM
    partial, fluid, to_right, to_left = call(
        first_kernel,
        "flux_step",
        place,
        [
            density.reshape(cells, width),
            momentum.reshape(3 * cells, width),
            energy.reshape(cells, width),
            solid_flags.reshape(cells, width),
        ],
        [(own, 2, None), (sends, 2, None)],
        [(5 * cells, width), (cells, width), (2, 5 * cells), (2, 5 * cells)],
        [pltpu.VMEM((5 * cells, width), jnp.float32)],
    )
    up = [(i, i + 1) for i in range(columns - 1)]
    down = [(i + 1, i) for i in range(columns - 1)]
    before = lax.ppermute(to_right, "gx", up)
    after = lax.ppermute(to_left, "gx", down)
    lines = 5 * planes
    advanced, summed, upper, lower = call(
        second_kernel,
        "advance_step",
        place,
        [partial, fluid, before, after],
        [(applied, 2, None), (ends, 0, smem)],
        [
            (5 * cells, width),
            (2 * lines, width),
            (reach * lines, width),
            (reach * lines, width),
        ],
    )
    low_rows = lax.ppermute(upper, "gy", [(i, i + 1) for i in range(parts - 1)])
    high_rows = lax.ppermute(lower, "gy", [(i + 1, i) for i in range(parts - 1)])
    near = [[g * inner + k for k in range(inner)] for g in range(outer)]
    far = [[g * inner + k for g in range(outer)] for k in range(inner)]
    gathered = lax.all_to_all(
        jnp.broadcast_to(summed[None], (inner, 2 * lines, width)),
        "gy",
        0,
        0,
        axis_index_groups=near,
    )
    prefix, slab = call(
        third_kernel,
        "group_step",
        place,
        [gathered],
        [(within, 0, smem)],
        [(2 * lines, width), (outer, lines, width)],
    )
    exchanged = lax.all_to_all(slab, "gy", 0, 0, axis_index_groups=far)
    (result,) = call(
        last_kernel,
        "filter_step",
        place,
        [advanced, fluid, low_rows, high_rows, prefix, exchanged],
        [(last, 0, smem)],
        [(5 * cells, width)],
    )
    return result.reshape(5, planes, transverse, width)


def solution(mesh):
    columns, parts = mesh.shape["gx"], mesh.shape["gy"]
    tables = streamwise_tables(columns, 1024 // columns) + tuple(
        transverse_tables(parts, 1536 // parts)
    )
    placed = (
        P(None, "gy", "gx"),
        P(None, None, "gy", "gx"),
        P(None, "gy", "gx"),
        P(None, "gy", "gx"),
    )
    return jax.shard_map(
        functools.partial(body, tables),
        mesh=mesh,
        in_specs=placed,
        out_specs=P(None, None, "gy", "gx"),
        check_vma=False,
    )
```

```python
import functools
import math

import jax
import jax.numpy as jnp
import numpy as np
from jax import lax
from jax.experimental import pallas as pl
from jax.experimental.pallas import tpu as pltpu
from jax.sharding import PartitionSpec as P

gas_gamma = 1.4
step_size = 0.1
filter_alpha = 0.4999
reach = 5
inner = 12
exact = lax.Precision.HIGHEST


def derivative_matrix(length):
    left = np.eye(length)
    right = np.zeros((length, length))
    for i in range(2, length - 2):
        left[i, i - 1] = left[i, i + 1] = 1.0 / 3.0
        right[i, i + 1], right[i, i - 1] = 7.0 / 9.0, -7.0 / 9.0
        right[i, i + 2], right[i, i - 2] = 1.0 / 36.0, -1.0 / 36.0
    left[0, 1] = 2.0
    right[0, :3] = -2.5, 2.0, 0.5
    left[1, 0] = left[1, 2] = 0.25
    right[1, 0], right[1, 2] = -0.75, 0.75
    left[-2, -3] = left[-2, -1] = 0.25
    right[-2, -3], right[-2, -1] = -0.75, 0.75
    left[-1, -2] = 2.0
    right[-1, -3:] = -0.5, -2.0, 2.5
    return np.linalg.solve(left, right)


def streamwise_tables(parts, width):
    whole = derivative_matrix(parts * width)
    rows = [slice(p * width, (p + 1) * width) for p in range(parts)]
    own = np.stack([whole[rows[p], rows[p]].T for p in range(parts)])
    sends = np.zeros((parts, 8, width))
    applied = np.zeros((parts, 8, width))
    for p in range(parts):
        if p + 1 < parts:
            block = whole[rows[p + 1], rows[p]]
            sends[p, 0:2] = block[0:2]
            applied[p + 1, 0, 0] = 1.0
            applied[p + 1, 1, 1:] = block[1:, -1] / block[1, -1]
        if p > 0:
            block = whole[rows[p - 1], rows[p]]
            sends[p, 2], sends[p, 3] = block[-1], block[-2]
            applied[p - 1, 2, -1] = 1.0
            applied[p - 1, 3, :-1] = block[:-1, 0] / block[-2, 0]
    return (
        (-step_size * own).astype(np.float32),
        sends.astype(np.float32),
        (-step_size * applied).astype(np.float32),
    )


def correction_matrix(length):
    count = length - 2 * reach
    left = np.eye(count)
    index = np.arange(count - 1)
    left[index, index + 1] = left[index + 1, index] = filter_alpha
    right = np.zeros((count, length))
    scale = (1.0 - 2.0 * filter_alpha) / 1024.0
    for shift in range(-reach, reach + 1):
        right[np.arange(count), np.arange(count) + reach + shift] = (
            scale * (-1.0) ** shift * math.comb(10, reach + shift)
        )
    whole = np.zeros((length, length))
    whole[reach : length - reach] = np.linalg.solve(left, right)
    return whole


def transverse_tables(parts, width):
    length = parts * width
    whole = correction_matrix(length)
    eta = math.acosh(0.5 / filter_alpha)

    def falling(ahead, behind):
        last = length - reach
        sign = (-1.0) ** (ahead - behind)
        return sign * math.sinh((last - ahead) * eta) / math.sinh((last - behind) * eta)

    def rising(ahead, behind):
        sign = (-1.0) ** (ahead - behind)
        return sign * math.sinh((ahead - reach + 1) * eta) / math.sinh((behind - reach + 1) * eta)

    outer = parts // inner
    own = np.zeros((parts, width, width + 2 * reach))
    up = np.zeros((parts, width))
    down = np.zeros((parts, width))
    from_low = np.zeros((parts, width))
    from_high = np.zeros((parts, width))
    for p in range(parts):
        start, end = p * width, (p + 1) * width - 1
        cells = slice(start, end + 1)
        if p + 1 < parts:
            up[p] = whole[end + 1 + reach, cells] * falling(end + 1, end + 1 + reach)
        if p > 0:
            down[p] = whole[start - 1 - reach, cells] * rising(start - 1, start - 1 - reach)
        for row in range(start, end + 1):
            if reach <= row < length - reach:
                from_low[p, row - start] = falling(row, start)
                from_high[p, row - start] = rising(row, end)
    for p in range(parts):
        start, end = p * width, (p + 1) * width - 1
        cells = slice(start, end + 1)
        own[p, :, reach : reach + width] = whole[cells, cells]
        if p > 0:
            near = whole[cells, start - reach : start]
            own[p, :, :reach] = near - np.outer(from_low[p], up[p - 1, -reach:])
        if p + 1 < parts:
            near = whole[cells, end + 1 : end + 1 + reach]
            own[p, :, reach + width :] = near - np.outer(from_high[p], down[p + 1, :reach])
    within = np.zeros((parts, 4, inner))
    across = np.zeros((parts, 2, outer))
    for p in range(parts):
        group, place = divmod(p, inner)
        start, end = p * width, (p + 1) * width - 1
        low_edge, high_edge = group * inner * width - 1, (group + 1) * inner * width
        for k in range(inner):
            q = group * inner + k
            if k < place:
                within[p, 0, k] = falling(start, (q + 1) * width)
            if k > place:
                within[p, 1, k] = rising(end, q * width - 1)
            if group + 1 < outer:
                within[p, 2, k] = falling(high_edge, (q + 1) * width)
            if group > 0:
                within[p, 3, k] = rising(low_edge, q * width - 1)
        for other in range(outer):
            if other < group:
                across[p, 0, other] = falling(start, (other + 1) * inner * width)
            if other > group:
                across[p, 1, other] = rising(end, other * inner * width - 1)
    ends = np.stack([up, down], axis=1)
    last = np.concatenate(
        [
            own.reshape(parts, -1),
            from_low,
            from_high,
            across.reshape(parts, -1),
        ],
        axis=1,
    )
    return [packed(table) for table in (ends, within, last)]


def packed(table):
    parts = table.shape[0]
    flat = table.reshape(parts, -1)
    room = -(-flat.shape[1] // 128) * 128
    wide = np.zeros((parts, 1, room), np.float32)
    wide[:, 0, : flat.shape[1]] = flat
    return wide


def first_kernel(density, momentum, energy, flags, partial, fluid, to_right, to_left, flux, table):
    planes, transverse = 8, 16
    cells = planes * transverse
    for j in range(transverse):
        picked = pl.ds(j, planes, stride=transverse)
        rho = density[picked, :]
        m0 = momentum[pl.ds(j, planes, stride=transverse), :]
        m1 = momentum[pl.ds(cells + j, planes, stride=transverse), :]
        m2 = momentum[pl.ds(2 * cells + j, planes, stride=transverse), :]
        total = energy[picked, :]
        row = pl.ds(j * planes, planes)
        fluid[row, :] = (1 - flags[picked, :]).astype(jnp.float32)
        inverse = 1.0 / rho
        velocity = m0 * inverse
        kinetic = 0.5 * (m0 * m0 + m1 * m1 + m2 * m2) * inverse
        pressure = (gas_gamma - 1.0) * (total - kinetic)
        fields = (
            m0,
            m0 * velocity + pressure,
            m1 * velocity,
            m2 * velocity,
            (total + pressure) * velocity,
        )
        for f, (held, moved) in enumerate(zip((rho, m0, m1, m2, total), fields)):
            at = pl.ds(f * cells + j * planes, planes)
            partial[at, :] = held
            flux[at, :] = moved
    own, sends = table(0), table(1)
    lines = flux[...]
    sent = lax.dot_general(
        sends[...], lines, (((1,), (1,)), ((), ())), precision=exact, preferred_element_type=jnp.float32
    )
    to_right[...] = sent[0:2]
    to_left[...] = sent[2:4]
    partial[...] = partial[...] + jnp.dot(
        lines, own[...], precision=exact, preferred_element_type=jnp.float32
    )


def second_kernel(partial, fluid, before, after, advanced, summed, upper, lower, table):
    planes, transverse = 8, 16
    cells = planes * transverse
    count = partial.shape[0]
    applied, ends = table(0), table(1)
    received = jnp.concatenate(
        [before[...], after[...], jnp.zeros((4, count), jnp.float32)], axis=0
    )
    added = lax.dot_general(
        received, applied[...], (((0,), (0,)), ((), ())), precision=exact, preferred_element_type=jnp.float32
    )
    state = partial[...] + added
    mask = fluid[...]
    for f in range(5):
        part = state[f * cells : (f + 1) * cells]
        if 1 <= f <= 3:
            part = part * mask
        advanced[f * cells : (f + 1) * cells, :] = part
        low, high = None, None
        for j in range(transverse):
            row = part[j * planes : (j + 1) * planes]
            one, two = ends[0, j] * row, ends[0, transverse + j] * row
            low = one if low is None else low + one
            high = two if high is None else high + two
        summed[f * planes : (f + 1) * planes, :] = low
        summed[(5 + f) * planes : (6 + f) * planes, :] = high
        width = reach * planes
        upper[f * width : (f + 1) * width, :] = part[cells - width :]
        lower[f * width : (f + 1) * width, :] = part[:width]


def third_kernel(gathered, prefix, slab, table):
    lines = gathered.shape[1] // 2
    outer = slab.shape[0]
    group = lax.axis_index("gy") // inner
    within = table(0)
    sums = []
    for kind in range(4):
        side = kind % 2
        total = None
        for k in range(inner):
            term = within[0, kind * inner + k] * gathered[k, side * lines : (side + 1) * lines, :]
            total = term if total is None else total + term
        sums.append(total)
    prefix[:lines, :] = sums[0]
    prefix[lines:, :] = sums[1]
    for other in range(outer):
        slab[other, :, :] = jnp.where(other > group, sums[2], sums[3])


def last_kernel(advanced, fluid, before, after, prefix, exchanged, result, table):
    planes, transverse = 8, 16
    cells = planes * transverse
    lines = 5 * planes
    outer = exchanged.shape[0]
    span = transverse + 2 * reach
    base = transverse * span
    weights = table(0)
    low, high = prefix[:lines, :], prefix[lines:, :]
    for other in range(outer):
        low = low + weights[0, base + 2 * transverse + other] * exchanged[other]
        high = high + weights[0, base + 2 * transverse + outer + other] * exchanged[other]
    width = reach * planes

    def cell(f, k):
        if k < reach:
            return before[f * width + k * planes : f * width + (k + 1) * planes, :]
        k -= reach
        if k < transverse:
            return advanced[f * cells + k * planes : f * cells + (k + 1) * planes, :]
        k -= transverse
        return after[f * width + k * planes : f * width + (k + 1) * planes, :]

    for i in range(transverse):
        falls, rises = weights[0, base + i], weights[0, base + transverse + i]
        sums = [
            falls * low[f * planes : (f + 1) * planes] + rises * high[f * planes : (f + 1) * planes]
            for f in range(5)
        ]
        for k in range(span):
            if k < reach and i >= reach or k >= reach + transverse and i < transverse - reach:
                continue
            weight = weights[0, i * span + k]
            sums = [total + weight * cell(f, k) for f, total in enumerate(sums)]
        keep = fluid[i * planes : (i + 1) * planes, :]
        for f in range(5):
            value = cell(f, reach + i) - sums[f]
            if 1 <= f <= 3:
                value = value * keep
            result[pl.ds(f * cells + i, planes, stride=transverse), :] = value


def call(kernel, name, arrays, tables, outs, scratch=(), inside=True, kept=True):
    given, held, made = len(arrays), len(tables), len(outs)

    def run(*refs):
        stored = refs[given : given + held]
        rest = refs[given + held : given + held + made]
        extra = refs[given + held + made : -held - 1]
        rows, sems = refs[-held - 1 : -1], refs[-1]
        copies = [
            pltpu.make_async_copy(stored[n].at[lax.axis_index(axis)], rows[n], sems.at[n])
            for n, (_, axis, _) in enumerate(tables)
        ]
        for copy in copies:
            copy.start()

        def table(n):
            copies[n].wait()
            return rows[n]

        kernel(*refs[:given], *rest, *extra, table)

    return pl.pallas_call(
        run,
        in_specs=[pl.BlockSpec(memory_space=pltpu.VMEM)] * given
        + [pl.BlockSpec(memory_space=pl.ANY)] * held,
        out_specs=[pl.BlockSpec(memory_space=pltpu.VMEM)] * made,
        out_shape=[
            pltpu.VMEM(shape, jnp.float32) if kept else jax.ShapeDtypeStruct(shape, jnp.float32)
            for shape in outs
        ],
        scratch_shapes=list(scratch)
        + [space(table.shape[1:], jnp.float32) for table, _, space in tables]
        + [pltpu.SemaphoreType.DMA((held,))],
        name=name,
    )(
        *[pltpu.with_memory_space_constraint(a, pltpu.VMEM) if inside else a for a in arrays],
        *[jnp.asarray(table) for table, _, _ in tables],
    )


def body(tables, density, momentum, energy, solid_flags):
    own, sends, applied, ends, within, last = tables
    planes, transverse, width = density.shape
    cells = planes * transverse
    parts, columns = lax.axis_size("gy"), lax.axis_size("gx")
    outer = parts // inner
    lines = 5 * planes
    partial, fluid, to_right, to_left = call(
        first_kernel,
        "flux_step",
        [
            density.reshape(cells, width),
            momentum.reshape(3 * cells, width),
            energy.reshape(cells, width),
            solid_flags.reshape(cells, width),
        ],
        [(own, "gx", pltpu.VMEM), (sends, "gx", pltpu.VMEM)],
        [(5 * cells, width), (cells, width), (2, 5 * cells), (2, 5 * cells)],
        [pltpu.VMEM((5 * cells, width), jnp.float32)],
        inside=False,
    )
    before = lax.ppermute(to_right, "gx", [(i, i + 1) for i in range(columns - 1)])
    after = lax.ppermute(to_left, "gx", [(i + 1, i) for i in range(columns - 1)])
    advanced, summed, upper, lower = call(
        second_kernel,
        "advance_step",
        [partial, fluid, before, after],
        [(applied, "gx", pltpu.VMEM), (ends, "gy", pltpu.SMEM)],
        [
            (5 * cells, width),
            (2 * lines, width),
            (reach * lines, width),
            (reach * lines, width),
        ],
    )
    low_rows = lax.ppermute(upper, "gy", [(i, i + 1) for i in range(parts - 1)])
    high_rows = lax.ppermute(lower, "gy", [(i + 1, i) for i in range(parts - 1)])
    near = [[g * inner + k for k in range(inner)] for g in range(outer)]
    far = [[g * inner + k for g in range(outer)] for k in range(inner)]
    gathered = lax.all_gather(summed, "gy", axis_index_groups=near)
    prefix, slab = call(
        third_kernel,
        "group_step",
        [gathered],
        [(within, "gy", pltpu.SMEM)],
        [(2 * lines, width), (outer, lines, width)],
    )
    exchanged = lax.all_to_all(slab, "gy", 0, 0, axis_index_groups=far)
    (result,) = call(
        last_kernel,
        "filter_step",
        [advanced, fluid, low_rows, high_rows, prefix, exchanged],
        [(last, "gy", pltpu.SMEM)],
        [(5 * cells, width)],
        kept=False,
    )
    return result.reshape(5, planes, transverse, width)


def solution(mesh):
    columns, parts = mesh.shape["gx"], mesh.shape["gy"]
    tables = streamwise_tables(columns, 1024 // columns) + tuple(
        transverse_tables(parts, 1536 // parts)
    )
    placed = (
        P(None, "gy", "gx"),
        P(None, None, "gy", "gx"),
        P(None, "gy", "gx"),
        P(None, "gy", "gx"),
    )
    return jax.shard_map(
        functools.partial(body, tables),
        mesh=mesh,
        in_specs=placed,
        out_specs=P(None, None, "gy", "gx"),
        check_vma=False,
    )
```

```python
import math

import jax
import jax.numpy as jnp
import numpy as np
from jax import lax
from jax.experimental import pallas as pl
from jax.experimental.pallas import tpu as pltpu
from jax.sharding import PartitionSpec as P

gas_gamma = 1.4
step_size = 0.1
filter_alpha = 0.4999
reach = 5
inner = 12
half = jnp.bfloat16


def derivative_matrix(length):
    left = np.eye(length)
    right = np.zeros((length, length))
    for i in range(2, length - 2):
        left[i, i - 1] = left[i, i + 1] = 1.0 / 3.0
        right[i, i + 1], right[i, i - 1] = 7.0 / 9.0, -7.0 / 9.0
        right[i, i + 2], right[i, i - 2] = 1.0 / 36.0, -1.0 / 36.0
    left[0, 1] = 2.0
    right[0, :3] = -2.5, 2.0, 0.5
    left[1, 0] = left[1, 2] = 0.25
    right[1, 0], right[1, 2] = -0.75, 0.75
    left[-2, -3] = left[-2, -1] = 0.25
    right[-2, -3], right[-2, -1] = -0.75, 0.75
    left[-1, -2] = 2.0
    right[-1, -3:] = -0.5, -2.0, 2.5
    return np.linalg.solve(left, right)


def halves(table):
    high = table.astype(np.float32).astype(half)
    low = (table - high.astype(np.float64)).astype(np.float32).astype(half)
    return high, low


def streamwise_tables(parts, width):
    whole = derivative_matrix(parts * width)
    rows = [slice(p * width, (p + 1) * width) for p in range(parts)]
    own = np.stack([whole[rows[p], rows[p]].T for p in range(parts)])
    sends = np.zeros((parts, 8, width))
    applied = np.zeros((parts, 4, width))
    for p in range(parts):
        above, below = (0, 2) if p % 2 == 0 else (2, 0)
        if p + 1 < parts:
            block = whole[rows[p + 1], rows[p]]
            sends[p, above : above + 2] = block[0:2]
            block = whole[rows[p], rows[p + 1]]
            applied[p, above, -1] = 1.0
            applied[p, above + 1, :-1] = block[:-1, 0] / block[-2, 0]
        if p > 0:
            block = whole[rows[p - 1], rows[p]]
            sends[p, below], sends[p, below + 1] = block[-1], block[-2]
            block = whole[rows[p], rows[p - 1]]
            applied[p, below, 0] = 1.0
            applied[p, below + 1, 1:] = block[1:, -1] / block[1, -1]
    high, low = halves(-step_size * applied)
    return (
        np.concatenate(halves(-step_size * own), axis=1),
        np.concatenate(halves(sends), axis=1),
        np.concatenate([high, high, low, np.zeros_like(low)], axis=1),
    )


def correction_matrix(length):
    count = length - 2 * reach
    left = np.eye(count)
    index = np.arange(count - 1)
    left[index, index + 1] = left[index + 1, index] = filter_alpha
    right = np.zeros((count, length))
    scale = (1.0 - 2.0 * filter_alpha) / 1024.0
    for shift in range(-reach, reach + 1):
        right[np.arange(count), np.arange(count) + reach + shift] = (
            scale * (-1.0) ** shift * math.comb(10, reach + shift)
        )
    whole = np.zeros((length, length))
    whole[reach : length - reach] = np.linalg.solve(left, right)
    return whole


def transverse_tables(parts, width):
    length = parts * width
    whole = correction_matrix(length)
    eta = math.acosh(0.5 / filter_alpha)

    def falling(ahead, behind):
        last = length - reach
        sign = (-1.0) ** (ahead - behind)
        return sign * math.sinh((last - ahead) * eta) / math.sinh((last - behind) * eta)

    def rising(ahead, behind):
        sign = (-1.0) ** (ahead - behind)
        return sign * math.sinh((ahead - reach + 1) * eta) / math.sinh((behind - reach + 1) * eta)

    outer = parts // inner
    own = np.zeros((parts, width, width + 2 * reach))
    up = np.zeros((parts, width))
    down = np.zeros((parts, width))
    from_low = np.zeros((parts, width))
    from_high = np.zeros((parts, width))
    for p in range(parts):
        start, end = p * width, (p + 1) * width - 1
        cells = slice(start, end + 1)
        if p + 1 < parts:
            up[p] = whole[end + 1 + reach, cells] * falling(end + 1, end + 1 + reach)
        if p > 0:
            down[p] = whole[start - 1 - reach, cells] * rising(start - 1, start - 1 - reach)
        for row in range(start, end + 1):
            if reach <= row < length - reach:
                from_low[p, row - start] = falling(row, start)
                from_high[p, row - start] = rising(row, end)
    for p in range(parts):
        start, end = p * width, (p + 1) * width - 1
        cells = slice(start, end + 1)
        own[p, :, reach : reach + width] = whole[cells, cells]
        if p > 0:
            near = whole[cells, start - reach : start]
            own[p, :, :reach] = near - np.outer(from_low[p], up[p - 1, -reach:])
        if p + 1 < parts:
            near = whole[cells, end + 1 : end + 1 + reach]
            own[p, :, reach + width :] = near - np.outer(from_high[p], down[p + 1, :reach])
    within = np.zeros((parts, 4, inner))
    across = np.zeros((parts, 2, outer))
    for p in range(parts):
        group, place = divmod(p, inner)
        start, end = p * width, (p + 1) * width - 1
        low_edge, high_edge = group * inner * width - 1, (group + 1) * inner * width
        for k in range(inner):
            q = group * inner + k
            if k < place:
                within[p, 0, k] = falling(start, (q + 1) * width)
            if k > place:
                within[p, 1, k] = rising(end, q * width - 1)
            if group + 1 < outer:
                within[p, 2, k] = falling(high_edge, (q + 1) * width)
            if group > 0:
                within[p, 3, k] = rising(low_edge, q * width - 1)
        for other in range(outer):
            if other < group:
                across[p, 0, other] = falling(start, (other + 1) * inner * width)
            if other > group:
                across[p, 1, other] = rising(end, other * inner * width - 1)
    ends = np.stack([up, down], axis=1)
    last = np.concatenate(
        [
            own.reshape(parts, -1),
            from_low,
            from_high,
            across.reshape(parts, -1),
        ],
        axis=1,
    )
    return [packed(table) for table in (ends, within, last)]


def packed(table):
    parts = table.shape[0]
    flat = table.reshape(parts, -1)
    room = -(-flat.shape[1] // 128) * 128
    wide = np.zeros((parts, 1, room), np.float32)
    wide[:, 0, : flat.shape[1]] = flat
    return wide


def first_kernel(
    density, momentum, energy, flags, partial, fluid, to_first, to_second, flux, table
):
    planes, transverse = 8, 16
    cells = planes * transverse
    for j in range(transverse):
        picked = pl.ds(j, planes, stride=transverse)
        rho = density[picked, :]
        m0 = momentum[pl.ds(j, planes, stride=transverse), :]
        m1 = momentum[pl.ds(cells + j, planes, stride=transverse), :]
        m2 = momentum[pl.ds(2 * cells + j, planes, stride=transverse), :]
        total = energy[picked, :]
        row = pl.ds(j * planes, planes)
        fluid[row, :] = (1 - flags[picked, :]).astype(jnp.float32)
        inverse = 1.0 / rho
        velocity = m0 * inverse
        kinetic = 0.5 * (m0 * m0 + m1 * m1 + m2 * m2) * inverse
        pressure = (gas_gamma - 1.0) * (total - kinetic)
        fields = (
            m0,
            m0 * velocity + pressure,
            m1 * velocity,
            m2 * velocity,
            (total + pressure) * velocity,
        )
        for f, (held, moved) in enumerate(zip((rho, m0, m1, m2, total), fields)):
            at = pl.ds(f * cells + j * planes, planes)
            partial[at, :] = held
            flux[at, :] = moved
    lines = flux[...]
    high = lines.astype(half)
    low = (lines - high.astype(jnp.float32)).astype(half)
    sends = table(1)[...]
    main, rest = (
        lax.dot_general(sends, part, (((1,), (1,)), ((), ())), preferred_element_type=jnp.float32)
        for part in (high, low)
    )
    sent = main[:8] + main[8:] + rest[:8]
    to_first[...] = sent[0:2]
    to_second[...] = sent[2:4]
    own = table(0)
    width = own.shape[1]
    coarse, fine = own[:width, :], own[width:, :]
    partial[...] = partial[...] + (
        jnp.dot(high, coarse, preferred_element_type=jnp.float32)
        + jnp.dot(high, fine, preferred_element_type=jnp.float32)
        + jnp.dot(low, coarse, preferred_element_type=jnp.float32)
    )


def second_kernel(partial, fluid, first, second, advanced, summed, first_rows, second_rows, table):
    planes, transverse = 8, 16
    cells = planes * transverse
    applied, ends = table(0), table(1)
    odd = lax.axis_index("gy") % 2 == 1
    received = jnp.concatenate([first[...], second[...]], axis=0)
    high = received.astype(half).astype(jnp.float32)
    stacked = jnp.concatenate([high, received - high, high, jnp.zeros_like(high)], axis=0)
    added = lax.dot_general(
        stacked.astype(half),
        applied[...],
        (((0,), (0,)), ((), ())),
        preferred_element_type=jnp.float32,
    )
    state = partial[...] + added
    mask = fluid[...]
    for f in range(5):
        part = state[f * cells : (f + 1) * cells]
        if 1 <= f <= 3:
            part = part * mask
        advanced[f * cells : (f + 1) * cells, :] = part
        low, high = None, None
        for j in range(transverse):
            row = part[j * planes : (j + 1) * planes]
            one, two = ends[0, j] * row, ends[0, transverse + j] * row
            low = one if low is None else low + one
            high = two if high is None else high + two
        summed[f * planes : (f + 1) * planes, :] = low
        summed[(5 + f) * planes : (6 + f) * planes, :] = high
        width = reach * planes
        at = slice(f * width, (f + 1) * width)
        first_rows[at, :] = jnp.where(odd, part[:width], part[cells - width :])
        second_rows[at, :] = jnp.where(odd, part[cells - width :], part[:width])


def third_kernel(gathered, prefix, slab, table):
    lines = gathered.shape[1] // 2
    outer = slab.shape[0]
    group = lax.axis_index("gy") // inner
    within = table(0)
    sums = []
    for kind in range(4):
        side = kind % 2
        total = None
        for k in range(inner):
            term = within[0, kind * inner + k] * gathered[k, side * lines : (side + 1) * lines, :]
            total = term if total is None else total + term
        sums.append(total)
    prefix[:lines, :] = sums[0]
    prefix[lines:, :] = sums[1]
    for other in range(outer):
        slab[other, :, :] = jnp.where(other > group, sums[2], sums[3])


def last_kernel(advanced, fluid, first, second, prefix, exchanged, result, table):
    planes, transverse = 8, 16
    cells = planes * transverse
    lines = 5 * planes
    outer = exchanged.shape[0]
    span = transverse + 2 * reach
    base = transverse * span
    weights = table(0)
    low, high = prefix[:lines, :], prefix[lines:, :]
    for other in range(outer):
        low = low + weights[0, base + 2 * transverse + other] * exchanged[other]
        high = high + weights[0, base + 2 * transverse + outer + other] * exchanged[other]
    width = reach * planes
    odd = lax.axis_index("gy") % 2 == 1

    def chosen(one, two, f, k):
        at = slice(f * width + k * planes, f * width + (k + 1) * planes)
        return jnp.where(odd, one[at, :], two[at, :])

    before = [[chosen(first, second, f, k) for k in range(reach)] for f in range(5)]
    after = [[chosen(second, first, f, k) for k in range(reach)] for f in range(5)]

    def cell(f, k):
        if k < reach:
            return before[f][k]
        k -= reach
        if k < transverse:
            return advanced[f * cells + k * planes : f * cells + (k + 1) * planes, :]
        return after[f][k - transverse]

    for i in range(transverse):
        falls, rises = weights[0, base + i], weights[0, base + transverse + i]
        sums = [
            falls * low[f * planes : (f + 1) * planes] + rises * high[f * planes : (f + 1) * planes]
            for f in range(5)
        ]
        for k in range(span):
            if k < reach and i >= reach or k >= reach + transverse and i < transverse - reach:
                continue
            weight = weights[0, i * span + k]
            sums = [total + weight * cell(f, k) for f, total in enumerate(sums)]
        keep = fluid[i * planes : (i + 1) * planes, :]
        for f in range(5):
            value = cell(f, reach + i) - sums[f]
            if 1 <= f <= 3:
                value = value * keep
            result[pl.ds(f * cells + i, planes, stride=transverse), :] = value


def call(kernel, arrays, tables, outs, scratch=(), inside=True, kept=True):
    given, held, made = len(arrays), len(tables), len(outs)

    def run(*refs):
        stored = refs[given : given + held]
        rest = refs[given + held : given + held + made]
        extra = refs[given + held + made : -held - 1]
        rows, sems = refs[-held - 1 : -1], refs[-1]
        copies = [
            pltpu.make_async_copy(stored[n].at[lax.axis_index(axis)], rows[n], sems.at[n])
            for n, (_, axis, _) in enumerate(tables)
        ]
        for copy in copies:
            copy.start()

        def table(n):
            copies[n].wait()
            return rows[n]

        kernel(*refs[:given], *rest, *extra, table)

    return pl.pallas_call(
        run,
        in_specs=[pl.BlockSpec(memory_space=pltpu.VMEM)] * given
        + [pl.BlockSpec(memory_space=pl.ANY)] * held,
        out_specs=[pl.BlockSpec(memory_space=pltpu.VMEM)] * made,
        out_shape=[
            pltpu.VMEM(shape, jnp.float32) if kept else jax.ShapeDtypeStruct(shape, jnp.float32)
            for shape in outs
        ],
        scratch_shapes=list(scratch)
        + [space(table.shape[1:], table.dtype) for table, _, space in tables]
        + [pltpu.SemaphoreType.DMA((held,))],
    )(
        *[pltpu.with_memory_space_constraint(a, pltpu.VMEM) if inside else a for a in arrays],
        *[jnp.asarray(table) for table, _, _ in tables],
    )


def pairs(start, count):
    swaps = []
    for i in range(start, count - 1, 2):
        swaps += [(i, i + 1), (i + 1, i)]
    return swaps


def body(tables, density, momentum, energy, solid_flags):
    own, sends, applied, ends, within, last = tables
    planes, transverse, width = density.shape
    cells = planes * transverse
    parts, columns = lax.axis_size("gy"), lax.axis_size("gx")
    outer = parts // inner
    lines = 5 * planes
    partial, fluid, to_first, to_second = call(
        first_kernel,
        [
            density.reshape(cells, width),
            momentum.reshape(3 * cells, width),
            energy.reshape(cells, width),
            solid_flags.reshape(cells, width),
        ],
        [(own, "gx", pltpu.VMEM), (sends, "gx", pltpu.VMEM)],
        [(5 * cells, width), (cells, width), (2, 5 * cells), (2, 5 * cells)],
        [pltpu.VMEM((5 * cells, width), jnp.float32)],
        inside=False,
    )
    second = lax.ppermute(to_second, "gx", pairs(1, columns))
    first = lax.ppermute(to_first, "gx", pairs(0, columns))
    advanced, summed, first_rows, second_rows = call(
        second_kernel,
        [partial, fluid, first, second],
        [(applied, "gx", pltpu.VMEM), (ends, "gy", pltpu.SMEM)],
        [
            (5 * cells, width),
            (2 * lines, width),
            (reach * lines, width),
            (reach * lines, width),
        ],
    )
    first_rows = lax.ppermute(first_rows, "gy", pairs(0, parts))
    second_rows = lax.ppermute(second_rows, "gy", pairs(1, parts))
    near = [[g * inner + k for k in range(inner)] for g in range(outer)]
    far = [[g * inner + k for g in range(outer)] for k in range(inner)]
    gathered = lax.all_gather(summed, "gy", axis_index_groups=near)
    prefix, slab = call(
        third_kernel,
        [gathered],
        [(within, "gy", pltpu.SMEM)],
        [(2 * lines, width), (outer, lines, width)],
    )
    exchanged = lax.all_to_all(slab, "gy", 0, 0, axis_index_groups=far)
    (result,) = call(
        last_kernel,
        [advanced, fluid, first_rows, second_rows, prefix, exchanged],
        [(last, "gy", pltpu.SMEM)],
        [(5 * cells, width)],
        kept=False,
    )
    return result.reshape(5, planes, transverse, width)


def solution(mesh):
    columns, parts = mesh.shape["gx"], mesh.shape["gy"]
    tables = streamwise_tables(columns, 1024 // columns) + tuple(
        transverse_tables(parts, 1536 // parts)
    )
    placed = (
        P(None, "gy", "gx"),
        P(None, None, "gy", "gx"),
        P(None, "gy", "gx"),
        P(None, "gy", "gx"),
    )

    def step(*arrays):
        return body(tables, *arrays)

    return jax.shard_map(
        step,
        mesh=mesh,
        in_specs=placed,
        out_specs=P(None, None, "gy", "gx"),
        check_vma=False,
    )
```

```python
import math

import jax
import jax.numpy as jnp
import numpy as np
from jax import lax
from jax.experimental import pallas as pl
from jax.experimental.pallas import tpu as pltpu
from jax.sharding import PartitionSpec as P

gas_gamma = 1.4
step_size = 0.1
filter_alpha = 0.4999
reach = 5
inner = 12
half = jnp.bfloat16


def derivative_matrix(length):
    left = np.eye(length)
    right = np.zeros((length, length))
    for i in range(2, length - 2):
        left[i, i - 1] = left[i, i + 1] = 1.0 / 3.0
        right[i, i + 1], right[i, i - 1] = 7.0 / 9.0, -7.0 / 9.0
        right[i, i + 2], right[i, i - 2] = 1.0 / 36.0, -1.0 / 36.0
    left[0, 1] = 2.0
    right[0, :3] = -2.5, 2.0, 0.5
    left[1, 0] = left[1, 2] = 0.25
    right[1, 0], right[1, 2] = -0.75, 0.75
    left[-2, -3] = left[-2, -1] = 0.25
    right[-2, -3], right[-2, -1] = -0.75, 0.75
    left[-1, -2] = 2.0
    right[-1, -3:] = -0.5, -2.0, 2.5
    return np.linalg.solve(left, right)


def halves(table):
    high = table.astype(np.float32).astype(half)
    low = (table - high.astype(np.float64)).astype(np.float32).astype(half)
    return high, low


def streamwise_tables(parts, width):
    whole = derivative_matrix(parts * width)
    rows = [slice(p * width, (p + 1) * width) for p in range(parts)]
    own = np.stack([whole[rows[p], rows[p]].T for p in range(parts)])
    sends = np.zeros((parts, 8, width))
    applied = np.zeros((parts, 4, width))
    for p in range(parts):
        above, below = (0, 2) if p % 2 == 0 else (2, 0)
        if p + 1 < parts:
            block = whole[rows[p + 1], rows[p]]
            sends[p, above : above + 2] = block[0:2]
            block = whole[rows[p], rows[p + 1]]
            applied[p, above, -1] = 1.0
            applied[p, above + 1, :-1] = block[:-1, 0] / block[-2, 0]
        if p > 0:
            block = whole[rows[p - 1], rows[p]]
            sends[p, below], sends[p, below + 1] = block[-1], block[-2]
            block = whole[rows[p], rows[p - 1]]
            applied[p, below, 0] = 1.0
            applied[p, below + 1, 1:] = block[1:, -1] / block[1, -1]
    high, low = halves(-step_size * applied)
    return (
        np.concatenate(halves(-step_size * own), axis=1),
        np.concatenate(halves(sends), axis=1),
        np.concatenate([high, high, low, np.zeros_like(low)], axis=1),
    )


def correction_matrix(length):
    count = length - 2 * reach
    left = np.eye(count)
    index = np.arange(count - 1)
    left[index, index + 1] = left[index + 1, index] = filter_alpha
    right = np.zeros((count, length))
    scale = (1.0 - 2.0 * filter_alpha) / 1024.0
    for shift in range(-reach, reach + 1):
        right[np.arange(count), np.arange(count) + reach + shift] = (
            scale * (-1.0) ** shift * math.comb(10, reach + shift)
        )
    whole = np.zeros((length, length))
    whole[reach : length - reach] = np.linalg.solve(left, right)
    return whole


def transverse_tables(parts, width):
    length = parts * width
    whole = correction_matrix(length)
    eta = math.acosh(0.5 / filter_alpha)

    def falling(ahead, behind):
        last = length - reach
        sign = (-1.0) ** (ahead - behind)
        return sign * math.sinh((last - ahead) * eta) / math.sinh((last - behind) * eta)

    def rising(ahead, behind):
        sign = (-1.0) ** (ahead - behind)
        return sign * math.sinh((ahead - reach + 1) * eta) / math.sinh((behind - reach + 1) * eta)

    outer = parts // inner
    own = np.zeros((parts, width, width + 2 * reach))
    up = np.zeros((parts, width))
    down = np.zeros((parts, width))
    from_low = np.zeros((parts, width))
    from_high = np.zeros((parts, width))
    for p in range(parts):
        start, end = p * width, (p + 1) * width - 1
        cells = slice(start, end + 1)
        if p + 1 < parts:
            up[p] = whole[end + 1 + reach, cells] * falling(end + 1, end + 1 + reach)
        if p > 0:
            down[p] = whole[start - 1 - reach, cells] * rising(start - 1, start - 1 - reach)
        for row in range(start, end + 1):
            if reach <= row < length - reach:
                from_low[p, row - start] = falling(row, start)
                from_high[p, row - start] = rising(row, end)
    for p in range(parts):
        start, end = p * width, (p + 1) * width - 1
        cells = slice(start, end + 1)
        own[p, :, reach : reach + width] = whole[cells, cells]
        if p > 0:
            near = whole[cells, start - reach : start]
            own[p, :, :reach] = near - np.outer(from_low[p], up[p - 1, -reach:])
        if p + 1 < parts:
            near = whole[cells, end + 1 : end + 1 + reach]
            own[p, :, reach + width :] = near - np.outer(from_high[p], down[p + 1, :reach])
    within = np.zeros((parts, 4, inner))
    across = np.zeros((parts, 2, outer))
    for p in range(parts):
        group, place = divmod(p, inner)
        start, end = p * width, (p + 1) * width - 1
        low_edge, high_edge = group * inner * width - 1, (group + 1) * inner * width
        for k in range(inner):
            q = group * inner + k
            if k < place:
                within[p, 0, k] = falling(start, (q + 1) * width)
            if k > place:
                within[p, 1, k] = rising(end, q * width - 1)
            if group + 1 < outer:
                within[p, 2, k] = falling(high_edge, (q + 1) * width)
            if group > 0:
                within[p, 3, k] = rising(low_edge, q * width - 1)
        for other in range(outer):
            if other < group:
                across[p, 0, other] = falling(start, (other + 1) * inner * width)
            if other > group:
                across[p, 1, other] = rising(end, other * inner * width - 1)
    ends = np.stack([up, down], axis=1)
    last = np.concatenate(
        [
            own.reshape(parts, -1),
            from_low,
            from_high,
            across.reshape(parts, -1),
        ],
        axis=1,
    )
    return [packed(table) for table in (ends, within, last)]


def packed(table):
    parts = table.shape[0]
    flat = table.reshape(parts, -1)
    room = -(-flat.shape[1] // 128) * 128
    wide = np.zeros((parts, 1, room), np.float32)
    wide[:, 0, : flat.shape[1]] = flat
    return wide


def first_kernel(
    density, momentum, energy, flags, partial, fluid, to_first, to_second, flux, table
):
    planes, transverse = 8, 16
    cells = planes * transverse
    for j in range(transverse):
        picked = pl.ds(j, planes, stride=transverse)
        rho = density[picked, :]
        m0 = momentum[pl.ds(j, planes, stride=transverse), :]
        m1 = momentum[pl.ds(cells + j, planes, stride=transverse), :]
        m2 = momentum[pl.ds(2 * cells + j, planes, stride=transverse), :]
        total = energy[picked, :]
        row = pl.ds(j * planes, planes)
        fluid[row, :] = (1 - flags[picked, :]).astype(jnp.float32)
        inverse = 1.0 / rho
        velocity = m0 * inverse
        kinetic = 0.5 * (m0 * m0 + m1 * m1 + m2 * m2) * inverse
        pressure = (gas_gamma - 1.0) * (total - kinetic)
        fields = (
            m0,
            m0 * velocity + pressure,
            m1 * velocity,
            m2 * velocity,
            (total + pressure) * velocity,
        )
        for f, (held, moved) in enumerate(zip((rho, m0, m1, m2, total), fields)):
            at = pl.ds(f * cells + j * planes, planes)
            partial[at, :] = held
            flux[at, :] = moved
    lines = flux[...]
    high = lines.astype(half)
    low = (lines - high.astype(jnp.float32)).astype(half)
    sends = table(1)[...]
    main, rest = (
        lax.dot_general(sends, part, (((1,), (1,)), ((), ())), preferred_element_type=jnp.float32)
        for part in (high, low)
    )
    sent = main[:8] + main[8:] + rest[:8]
    to_first[...] = sent[0:2]
    to_second[...] = sent[2:4]
    own = table(0)
    width = own.shape[1]
    coarse, fine = own[:width, :], own[width:, :]
    partial[...] = partial[...] + (
        jnp.dot(high, coarse, preferred_element_type=jnp.float32)
        + jnp.dot(high, fine, preferred_element_type=jnp.float32)
        + jnp.dot(low, coarse, preferred_element_type=jnp.float32)
    )


def second_kernel(partial, fluid, first, second, advanced, summed, first_rows, second_rows, table):
    planes, transverse = 8, 16
    cells = planes * transverse
    applied, ends = table(0), table(1)
    odd = lax.axis_index("gy") % 2 == 1
    received = jnp.concatenate([first[...], second[...]], axis=0)
    high = received.astype(half).astype(jnp.float32)
    stacked = jnp.concatenate([high, received - high, high, jnp.zeros_like(high)], axis=0)
    added = lax.dot_general(
        stacked.astype(half),
        applied[...],
        (((0,), (0,)), ((), ())),
        preferred_element_type=jnp.float32,
    )
    state = partial[...] + added
    mask = fluid[...]
    for f in range(5):
        part = state[f * cells : (f + 1) * cells]
        if 1 <= f <= 3:
            part = part * mask
        advanced[f * cells : (f + 1) * cells, :] = part
        low, high = None, None
        for j in range(transverse):
            row = part[j * planes : (j + 1) * planes]
            one, two = ends[0, j] * row, ends[0, transverse + j] * row
            low = one if low is None else low + one
            high = two if high is None else high + two
        summed[f * planes : (f + 1) * planes, :] = low
        summed[(5 + f) * planes : (6 + f) * planes, :] = high
        width = reach * planes
        at = slice(f * width, (f + 1) * width)
        first_rows[at, :] = jnp.where(odd, part[:width], part[cells - width :])
        second_rows[at, :] = jnp.where(odd, part[cells - width :], part[:width])


def third_kernel(gathered, prefix, slab, table):
    lines = gathered.shape[1] // 2
    outer = slab.shape[0]
    group = lax.axis_index("gy") // inner
    within = table(0)
    sums = []
    for kind in range(4):
        side = kind % 2
        total = None
        for k in range(inner):
            term = within[0, kind * inner + k] * gathered[k, side * lines : (side + 1) * lines, :]
            total = term if total is None else total + term
        sums.append(total)
    prefix[:lines, :] = sums[0]
    prefix[lines:, :] = sums[1]
    for other in range(outer):
        slab[other, :, :] = jnp.where(other > group, sums[2], sums[3])


def last_kernel(advanced, fluid, first, second, prefix, exchanged, result, table):
    planes, transverse = 8, 16
    cells = planes * transverse
    lines = 5 * planes
    outer = exchanged.shape[0]
    span = transverse + 2 * reach
    base = transverse * span
    weights = table(0)
    low, high = prefix[:lines, :], prefix[lines:, :]
    for other in range(outer):
        low = low + weights[0, base + 2 * transverse + other] * exchanged[other]
        high = high + weights[0, base + 2 * transverse + outer + other] * exchanged[other]
    width = reach * planes
    odd = lax.axis_index("gy") % 2 == 1

    def chosen(one, two, f, k):
        at = slice(f * width + k * planes, f * width + (k + 1) * planes)
        return jnp.where(odd, one[at, :], two[at, :])

    before = [[chosen(first, second, f, k) for k in range(reach)] for f in range(5)]
    after = [[chosen(second, first, f, k) for k in range(reach)] for f in range(5)]

    def cell(f, k):
        if k < reach:
            return before[f][k]
        k -= reach
        if k < transverse:
            return advanced[f * cells + k * planes : f * cells + (k + 1) * planes, :]
        return after[f][k - transverse]

    for i in range(transverse):
        falls, rises = weights[0, base + i], weights[0, base + transverse + i]
        sums = [
            falls * low[f * planes : (f + 1) * planes] + rises * high[f * planes : (f + 1) * planes]
            for f in range(5)
        ]
        for k in range(span):
            if k < reach and i >= reach or k >= reach + transverse and i < transverse - reach:
                continue
            weight = weights[0, i * span + k]
            sums = [total + weight * cell(f, k) for f, total in enumerate(sums)]
        keep = fluid[i * planes : (i + 1) * planes, :]
        for f in range(5):
            value = cell(f, reach + i) - sums[f]
            if 1 <= f <= 3:
                value = value * keep
            result[pl.ds(f * cells + i, planes, stride=transverse), :] = value


def call(kernel, arrays, tables, outs, scratch=(), rows=(), ahead=(), inside=True, kept=True):
    given, held, made = len(arrays) + len(rows), len(tables) + len(ahead), len(outs)

    def run(*refs):
        stored = refs[given : given + held]
        rest = refs[given + held : given + held + made]
        put = refs[given + held + made : given + held + made + len(ahead)]
        extra = refs[given + held + made + len(ahead) : len(refs) - 1 - len(tables)]
        extra, sems = (extra, refs[-1]) if held else (refs[given + held + made :], None)
        placed = (*refs[len(refs) - 1 - len(tables) : -1], *put)
        copies = [
            pltpu.make_async_copy(stored[n].at[lax.axis_index(axis)], placed[n], sems.at[n])
            for n, (_, axis) in enumerate([t[:2] for t in tables] + [t[:2] for t in ahead])
        ]
        for copy in copies:
            copy.start()

        def table(n):
            if n >= len(tables):
                return refs[len(arrays) + n - len(tables)]
            copies[n].wait()
            return placed[n]

        kernel(*refs[: len(arrays)], *rest, *extra, table)
        for copy in copies[len(tables) :]:
            copy.wait()

    vmem, smem = pl.BlockSpec(memory_space=pltpu.VMEM), pl.BlockSpec(memory_space=pltpu.SMEM)
    return pl.pallas_call(
        run,
        in_specs=[vmem] * len(arrays) + [smem] * len(rows) + [pl.BlockSpec(memory_space=pl.ANY)] * held,
        out_specs=[vmem] * made + [smem] * len(ahead),
        out_shape=[
            pltpu.VMEM(shape, jnp.float32) if kept else jax.ShapeDtypeStruct(shape, jnp.float32)
            for shape in outs
        ]
        + [pltpu.SMEM(table.shape[1:], jnp.float32) for table, _ in ahead],
        scratch_shapes=list(scratch)
        + [space(table.shape[1:], table.dtype) for table, _, space in tables]
        + ([pltpu.SemaphoreType.DMA((held,))] if held else []),
    )(
        *[pltpu.with_memory_space_constraint(a, pltpu.VMEM) if inside else a for a in arrays],
        *[pltpu.with_memory_space_constraint(row, pltpu.SMEM) for row in rows],
        *[jnp.asarray(t[0]) for t in (*tables, *ahead)],
    )


def pairs(start, count):
    swaps = []
    for i in range(start, count - 1, 2):
        swaps += [(i, i + 1), (i + 1, i)]
    return swaps


def body(tables, density, momentum, energy, solid_flags):
    own, sends, applied, ends, within, last = tables
    planes, transverse, width = density.shape
    cells = planes * transverse
    parts, columns = lax.axis_size("gy"), lax.axis_size("gx")
    outer = parts // inner
    lines = 5 * planes
    partial, fluid, to_first, to_second, within_row, last_row = call(
        first_kernel,
        [
            density.reshape(cells, width),
            momentum.reshape(3 * cells, width),
            energy.reshape(cells, width),
            solid_flags.reshape(cells, width),
        ],
        [(own, "gx", pltpu.VMEM), (sends, "gx", pltpu.VMEM)],
        [(5 * cells, width), (cells, width), (2, 5 * cells), (2, 5 * cells)],
        [pltpu.VMEM((5 * cells, width), jnp.float32)],
        ahead=[(within, "gy"), (last, "gy")],
        inside=False,
    )
    second = lax.ppermute(to_second, "gx", pairs(1, columns))
    first = lax.ppermute(to_first, "gx", pairs(0, columns))
    advanced, summed, first_rows, second_rows = call(
        second_kernel,
        [partial, fluid, first, second],
        [(applied, "gx", pltpu.VMEM), (ends, "gy", pltpu.SMEM)],
        [
            (5 * cells, width),
            (2 * lines, width),
            (reach * lines, width),
            (reach * lines, width),
        ],
    )
    first_rows = lax.ppermute(first_rows, "gy", pairs(0, parts))
    second_rows = lax.ppermute(second_rows, "gy", pairs(1, parts))
    near = [[g * inner + k for k in range(inner)] for g in range(outer)]
    far = [[g * inner + k for g in range(outer)] for k in range(inner)]
    gathered = lax.all_gather(summed, "gy", axis_index_groups=near)
    prefix, slab = call(
        third_kernel, [gathered], [], [(2 * lines, width), (outer, lines, width)], rows=[within_row]
    )
    exchanged = lax.all_to_all(slab, "gy", 0, 0, axis_index_groups=far)
    (result,) = call(
        last_kernel,
        [advanced, fluid, first_rows, second_rows, prefix, exchanged],
        [],
        [(5 * cells, width)],
        rows=[last_row],
        kept=False,
    )
    return result.reshape(5, planes, transverse, width)


def solution(mesh):
    columns, parts = mesh.shape["gx"], mesh.shape["gy"]
    tables = streamwise_tables(columns, 1024 // columns) + tuple(
        transverse_tables(parts, 1536 // parts)
    )
    placed = (
        P(None, "gy", "gx"),
        P(None, None, "gy", "gx"),
        P(None, "gy", "gx"),
        P(None, "gy", "gx"),
    )

    def step(*arrays):
        return body(tables, *arrays)

    return jax.shard_map(
        step,
        mesh=mesh,
        in_specs=placed,
        out_specs=P(None, None, "gy", "gx"),
        check_vma=False,
    )
```

```python
import math

import jax
import jax.numpy as jnp
import numpy as np
from jax import lax
from jax.experimental import pallas as pl
from jax.experimental.pallas import tpu as pltpu
from jax.sharding import PartitionSpec as P

gas_gamma = 1.4
step_size = 0.1
filter_alpha = 0.4999
reach = 5
inner = 12
half = jnp.bfloat16


def derivative_matrix(length):
    left = np.eye(length)
    right = np.zeros((length, length))
    for i in range(2, length - 2):
        left[i, i - 1] = left[i, i + 1] = 1.0 / 3.0
        right[i, i + 1], right[i, i - 1] = 7.0 / 9.0, -7.0 / 9.0
        right[i, i + 2], right[i, i - 2] = 1.0 / 36.0, -1.0 / 36.0
    left[0, 1] = 2.0
    right[0, :3] = -2.5, 2.0, 0.5
    left[1, 0] = left[1, 2] = 0.25
    right[1, 0], right[1, 2] = -0.75, 0.75
    left[-2, -3] = left[-2, -1] = 0.25
    right[-2, -3], right[-2, -1] = -0.75, 0.75
    left[-1, -2] = 2.0
    right[-1, -3:] = -0.5, -2.0, 2.5
    return np.linalg.solve(left, right)


def halves(table):
    high = table.astype(np.float32).astype(half)
    low = (table - high.astype(np.float64)).astype(np.float32).astype(half)
    return high, low


def streamwise_tables(parts, width):
    whole = derivative_matrix(parts * width)
    rows = [slice(p * width, (p + 1) * width) for p in range(parts)]
    own = np.stack([whole[rows[p], rows[p]].T for p in range(parts)])
    sends = np.zeros((parts, 8, width))
    applied = np.zeros((parts, 4, width))
    for p in range(parts):
        above, below = (0, 2) if p % 2 == 0 else (2, 0)
        if p + 1 < parts:
            block = whole[rows[p + 1], rows[p]]
            sends[p, above : above + 2] = block[0:2]
            block = whole[rows[p], rows[p + 1]]
            applied[p, above, -1] = 1.0
            applied[p, above + 1, :-1] = block[:-1, 0] / block[-2, 0]
        if p > 0:
            block = whole[rows[p - 1], rows[p]]
            sends[p, below], sends[p, below + 1] = block[-1], block[-2]
            block = whole[rows[p], rows[p - 1]]
            applied[p, below, 0] = 1.0
            applied[p, below + 1, 1:] = block[1:, -1] / block[1, -1]
    high, low = halves(-step_size * applied)
    return (
        np.concatenate(halves(-step_size * own), axis=1),
        np.concatenate(halves(sends), axis=1),
        np.concatenate([high, high, low, np.zeros_like(low)], axis=1),
    )


def correction_matrix(length):
    count = length - 2 * reach
    left = np.eye(count)
    index = np.arange(count - 1)
    left[index, index + 1] = left[index + 1, index] = filter_alpha
    right = np.zeros((count, length))
    scale = (1.0 - 2.0 * filter_alpha) / 1024.0
    for shift in range(-reach, reach + 1):
        right[np.arange(count), np.arange(count) + reach + shift] = (
            scale * (-1.0) ** shift * math.comb(10, reach + shift)
        )
    whole = np.zeros((length, length))
    whole[reach : length - reach] = np.linalg.solve(left, right)
    return whole


def transverse_tables(parts, width):
    length = parts * width
    whole = correction_matrix(length)
    eta = math.acosh(0.5 / filter_alpha)

    def falling(ahead, behind):
        last = length - reach
        sign = (-1.0) ** (ahead - behind)
        return sign * math.sinh((last - ahead) * eta) / math.sinh((last - behind) * eta)

    def rising(ahead, behind):
        sign = (-1.0) ** (ahead - behind)
        return sign * math.sinh((ahead - reach + 1) * eta) / math.sinh((behind - reach + 1) * eta)

    outer = parts // inner
    own = np.zeros((parts, width, width + 2 * reach))
    up = np.zeros((parts, width))
    down = np.zeros((parts, width))
    from_low = np.zeros((parts, width))
    from_high = np.zeros((parts, width))
    for p in range(parts):
        start, end = p * width, (p + 1) * width - 1
        cells = slice(start, end + 1)
        if p + 1 < parts:
            up[p] = whole[end + 1 + reach, cells] * falling(end + 1, end + 1 + reach)
        if p > 0:
            down[p] = whole[start - 1 - reach, cells] * rising(start - 1, start - 1 - reach)
        for row in range(start, end + 1):
            if reach <= row < length - reach:
                from_low[p, row - start] = falling(row, start)
                from_high[p, row - start] = rising(row, end)
    for p in range(parts):
        start, end = p * width, (p + 1) * width - 1
        cells = slice(start, end + 1)
        own[p, :, reach : reach + width] = whole[cells, cells]
        if p > 0:
            near = whole[cells, start - reach : start]
            own[p, :, :reach] = near - np.outer(from_low[p], up[p - 1, -reach:])
        if p + 1 < parts:
            near = whole[cells, end + 1 : end + 1 + reach]
            own[p, :, reach + width :] = near - np.outer(from_high[p], down[p + 1, :reach])
    within = np.zeros((parts, 4, inner))
    across = np.zeros((parts, 2, outer))
    for p in range(parts):
        group, place = divmod(p, inner)
        start, end = p * width, (p + 1) * width - 1
        low_edge, high_edge = group * inner * width - 1, (group + 1) * inner * width
        for k in range(inner):
            q = group * inner + k
            if k < place:
                within[p, 0, k] = falling(start, (q + 1) * width)
            if k > place:
                within[p, 1, k] = rising(end, q * width - 1)
            if group + 1 < outer:
                within[p, 2, k] = falling(high_edge, (q + 1) * width)
            if group > 0:
                within[p, 3, k] = rising(low_edge, q * width - 1)
        for other in range(outer):
            if other < group:
                across[p, 0, other] = falling(start, (other + 1) * inner * width)
            if other > group:
                across[p, 1, other] = rising(end, other * inner * width - 1)
    ends = np.stack([up, down], axis=1)
    last = np.concatenate(
        [
            own.reshape(parts, -1),
            from_low,
            from_high,
            across.reshape(parts, -1),
        ],
        axis=1,
    )
    return [packed(table) for table in (ends, within, last)]


def packed(table):
    parts = table.shape[0]
    flat = table.reshape(parts, -1)
    room = -(-flat.shape[1] // 128) * 128
    wide = np.zeros((parts, 1, room), np.float32)
    wide[:, 0, : flat.shape[1]] = flat
    return wide


def first_kernel(
    density, momentum, energy, flags, partial, fluid, to_first, to_second, flux, table
):
    planes, transverse = 8, 16
    cells = planes * transverse
    for j in range(transverse):
        picked = pl.ds(j, planes, stride=transverse)
        rho = density[picked, :]
        m0 = momentum[pl.ds(j, planes, stride=transverse), :]
        m1 = momentum[pl.ds(cells + j, planes, stride=transverse), :]
        m2 = momentum[pl.ds(2 * cells + j, planes, stride=transverse), :]
        total = energy[picked, :]
        row = pl.ds(j * planes, planes)
        fluid[row, :] = (1 - flags[picked, :]).astype(jnp.float32)
        inverse = 1.0 / rho
        velocity = m0 * inverse
        kinetic = 0.5 * (m0 * m0 + m1 * m1 + m2 * m2) * inverse
        pressure = (gas_gamma - 1.0) * (total - kinetic)
        fields = (
            m0,
            m0 * velocity + pressure,
            m1 * velocity,
            m2 * velocity,
            (total + pressure) * velocity,
        )
        for f, (held, moved) in enumerate(zip((rho, m0, m1, m2, total), fields)):
            at = pl.ds(f * cells + j * planes, planes)
            partial[at, :] = held
            flux[at, :] = moved
    lines = flux[...]
    high = lines.astype(half)
    low = (lines - high.astype(jnp.float32)).astype(half)
    sends = table(1)[...]
    main, rest = (
        lax.dot_general(sends, part, (((1,), (1,)), ((), ())), preferred_element_type=jnp.float32)
        for part in (high, low)
    )
    sent = main[:8] + main[8:] + rest[:8]
    to_first[...] = sent[0:2]
    to_second[...] = sent[2:4]
    own = table(0)
    width = own.shape[1]
    coarse, fine = own[:width, :], own[width:, :]
    partial[...] = partial[...] + (
        jnp.dot(high, coarse, preferred_element_type=jnp.float32)
        + jnp.dot(high, fine, preferred_element_type=jnp.float32)
        + jnp.dot(low, coarse, preferred_element_type=jnp.float32)
    )


def second_kernel(partial, fluid, first, second, advanced, summed, first_rows, second_rows, table):
    planes, transverse = 8, 16
    cells = planes * transverse
    applied, ends = table(0), table(1)
    odd = lax.axis_index("gy") % 2 == 1
    received = jnp.concatenate([first[...], second[...]], axis=0)
    high = received.astype(half).astype(jnp.float32)
    stacked = jnp.concatenate([high, received - high, high, jnp.zeros_like(high)], axis=0)
    added = lax.dot_general(
        stacked.astype(half),
        applied[...],
        (((0,), (0,)), ((), ())),
        preferred_element_type=jnp.float32,
    )
    state = partial[...] + added
    mask = fluid[...]
    for f in range(5):
        part = state[f * cells : (f + 1) * cells]
        if 1 <= f <= 3:
            part = part * mask
        advanced[f * cells : (f + 1) * cells, :] = part
        low, high = None, None
        for j in range(transverse):
            row = part[j * planes : (j + 1) * planes]
            one, two = ends[0, j] * row, ends[0, transverse + j] * row
            low = one if low is None else low + one
            high = two if high is None else high + two
        summed[f * planes : (f + 1) * planes, :] = low
        summed[(5 + f) * planes : (6 + f) * planes, :] = high
        width = reach * planes
        at = slice(f * width, (f + 1) * width)
        first_rows[at, :] = jnp.where(odd, part[:width], part[cells - width :])
        second_rows[at, :] = jnp.where(odd, part[cells - width :], part[:width])


def third_kernel(gathered, prefix, slab, table):
    lines = gathered.shape[1] // 2
    outer = slab.shape[0]
    group = lax.axis_index("gy") // inner
    within = table(0)
    sums = []
    for kind in range(4):
        side = kind % 2
        total = None
        for k in range(inner):
            term = within[0, kind * inner + k] * gathered[k, side * lines : (side + 1) * lines, :]
            total = term if total is None else total + term
        sums.append(total)
    prefix[:lines, :] = sums[0]
    prefix[lines:, :] = sums[1]
    for other in range(outer):
        slab[other, :, :] = jnp.where(other > group, sums[2], sums[3])


def last_kernel(advanced, fluid, first, second, prefix, exchanged, result, table):
    planes, transverse = 8, 16
    cells = planes * transverse
    lines = 5 * planes
    outer = exchanged.shape[0]
    span = transverse + 2 * reach
    base = transverse * span
    weights = table(0)
    low, high = prefix[:lines, :], prefix[lines:, :]
    for other in range(outer):
        low = low + weights[0, base + 2 * transverse + other] * exchanged[other]
        high = high + weights[0, base + 2 * transverse + outer + other] * exchanged[other]
    width = reach * planes
    odd = lax.axis_index("gy") % 2 == 1

    def chosen(one, two, f, k):
        at = slice(f * width + k * planes, f * width + (k + 1) * planes)
        return jnp.where(odd, one[at, :], two[at, :])

    before = [[chosen(first, second, f, k) for k in range(reach)] for f in range(5)]
    after = [[chosen(second, first, f, k) for k in range(reach)] for f in range(5)]

    def cell(f, k):
        if k < reach:
            return before[f][k]
        k -= reach
        if k < transverse:
            return advanced[f * cells + k * planes : f * cells + (k + 1) * planes, :]
        return after[f][k - transverse]

    for i in range(transverse):
        falls, rises = weights[0, base + i], weights[0, base + transverse + i]
        sums = [
            falls * low[f * planes : (f + 1) * planes] + rises * high[f * planes : (f + 1) * planes]
            for f in range(5)
        ]
        for k in range(span):
            if k < reach and i >= reach or k >= reach + transverse and i < transverse - reach:
                continue
            weight = weights[0, i * span + k]
            sums = [total + weight * cell(f, k) for f, total in enumerate(sums)]
        keep = fluid[i * planes : (i + 1) * planes, :]
        for f in range(5):
            value = cell(f, reach + i) - sums[f]
            if 1 <= f <= 3:
                value = value * keep
            result[pl.ds(f * cells + i, planes, stride=transverse), :] = value


def call(kernel, arrays, tables, outs, scratch=(), rows=(), ahead=(), inside=True, kept=True):
    given, held, made = len(arrays) + len(rows), len(tables) + len(ahead), len(outs)

    def run(*refs):
        stored = refs[given : given + held]
        rest = refs[given + held : given + held + made]
        put = refs[given + held + made : given + held + made + len(ahead)]
        extra = refs[given + held + made + len(ahead) : len(refs) - 1 - len(tables)]
        extra, sems = (extra, refs[-1]) if held else (refs[given + held + made :], None)
        placed = (*refs[len(refs) - 1 - len(tables) : -1], *put)
        copies = [
            pltpu.make_async_copy(stored[n].at[lax.axis_index(axis)], placed[n], sems.at[n])
            for n, (_, axis) in enumerate([t[:2] for t in tables] + [t[:2] for t in ahead])
        ]
        for copy in copies:
            copy.start()

        def table(n):
            if n >= len(tables):
                return refs[len(arrays) + n - len(tables)]
            copies[n].wait()
            return placed[n]

        kernel(*refs[: len(arrays)], *rest, *extra, table)
        for copy in copies[len(tables) :]:
            copy.wait()

    vmem = pl.BlockSpec(memory_space=pltpu.VMEM)
    return pl.pallas_call(
        run,
        in_specs=[vmem] * len(arrays)
        + [pl.BlockSpec(memory_space=space) for _, space in rows]
        + [pl.BlockSpec(memory_space=pl.ANY)] * held,
        out_specs=[vmem] * made + [pl.BlockSpec(memory_space=space) for _, _, space in ahead],
        out_shape=[
            pltpu.VMEM(shape, jnp.float32) if kept else jax.ShapeDtypeStruct(shape, jnp.float32)
            for shape in outs
        ]
        + [space(table.shape[1:], table.dtype) for table, _, space in ahead],
        scratch_shapes=list(scratch)
        + [space(table.shape[1:], table.dtype) for table, _, space in tables]
        + ([pltpu.SemaphoreType.DMA((held,))] if held else []),
    )(
        *[pltpu.with_memory_space_constraint(a, pltpu.VMEM) if inside else a for a in arrays],
        *[pltpu.with_memory_space_constraint(row, space) for row, space in rows],
        *[jnp.asarray(t[0]) for t in (*tables, *ahead)],
    )


def pairs(start, count):
    swaps = []
    for i in range(start, count - 1, 2):
        swaps += [(i, i + 1), (i + 1, i)]
    return swaps


def body(tables, density, momentum, energy, solid_flags):
    own, sends, applied, ends, within, last = tables
    planes, transverse, width = density.shape
    cells = planes * transverse
    parts, columns = lax.axis_size("gy"), lax.axis_size("gx")
    outer = parts // inner
    lines = 5 * planes
    partial, fluid, to_first, to_second, *fetched = call(
        first_kernel,
        [
            density.reshape(cells, width),
            momentum.reshape(3 * cells, width),
            energy.reshape(cells, width),
            solid_flags.reshape(cells, width),
        ],
        [(own, "gx", pltpu.VMEM), (sends, "gx", pltpu.VMEM)],
        [(5 * cells, width), (cells, width), (2, 5 * cells), (2, 5 * cells)],
        [pltpu.VMEM((5 * cells, width), jnp.float32)],
        ahead=[
            (applied, "gx", pltpu.VMEM),
            (ends, "gy", pltpu.SMEM),
            (within, "gy", pltpu.SMEM),
            (last, "gy", pltpu.SMEM),
        ],
        inside=False,
    )
    second = lax.ppermute(to_second, "gx", pairs(1, columns))
    first = lax.ppermute(to_first, "gx", pairs(0, columns))
    advanced, summed, first_rows, second_rows = call(
        second_kernel,
        [partial, fluid, first, second],
        [],
        [
            (5 * cells, width),
            (2 * lines, width),
            (reach * lines, width),
            (reach * lines, width),
        ],
        rows=[(fetched[0], pltpu.VMEM), (fetched[1], pltpu.SMEM)],
    )
    first_rows = lax.ppermute(first_rows, "gy", pairs(0, parts))
    second_rows = lax.ppermute(second_rows, "gy", pairs(1, parts))
    near = [[g * inner + k for k in range(inner)] for g in range(outer)]
    far = [[g * inner + k for g in range(outer)] for k in range(inner)]
    gathered = lax.all_gather(summed, "gy", axis_index_groups=near)
    prefix, slab = call(
        third_kernel,
        [gathered],
        [],
        [(2 * lines, width), (outer, lines, width)],
        rows=[(fetched[2], pltpu.SMEM)],
    )
    exchanged = lax.all_to_all(slab, "gy", 0, 0, axis_index_groups=far)
    (result,) = call(
        last_kernel,
        [advanced, fluid, first_rows, second_rows, prefix, exchanged],
        [],
        [(5 * cells, width)],
        rows=[(fetched[3], pltpu.SMEM)],
        kept=False,
    )
    return result.reshape(5, planes, transverse, width)


def solution(mesh):
    columns, parts = mesh.shape["gx"], mesh.shape["gy"]
    tables = streamwise_tables(columns, 1024 // columns) + tuple(
        transverse_tables(parts, 1536 // parts)
    )
    placed = (
        P(None, "gy", "gx"),
        P(None, None, "gy", "gx"),
        P(None, "gy", "gx"),
        P(None, "gy", "gx"),
    )

    def step(*arrays):
        return body(tables, *arrays)

    return jax.shard_map(
        step,
        mesh=mesh,
        in_specs=placed,
        out_specs=P(None, None, "gy", "gx"),
        check_vma=False,
    )
```
